32 devices in a mesh: area: 4 (over y, x), scen: 8 (over z, core).
Axes of the slice: x: 2, y: 2, z: 4, core: 2. Of those that a mesh axis runs over, the one named last changes fastest.
Arguments:
- load: float32 [64, 12, 8192], P('scen', None, 'area'), may hold values from -6 to 6
- start: float32 [64, 12, 8192], P('scen', None, 'area'), may hold values from -6 to 6
- multipliers: float32 [64, 12, 1024], P('scen', None, 'area'), may hold values from -4 to 4
- weights: float32 [64], P('scen'), may hold values from 0.25 to 4
- penalty: float32 [1024], P('area'), may hold values from 0.3 to 3
- inverse: bfloat16 [8192, 2048], P('area'), may hold values from -1 to 2
- ports: int32 [4, 128], replicated, may hold values from 0 to 2047
- neighbour: int32 [4, 4], replicated, may hold values from 0 to 3, as said below
- remote_port: int32 [4, 4, 32], replicated, may hold values from 0 to 127
- local_bus: int32 [4, 4, 32], replicated, may hold values from 0 to 2047
- susceptance: float32 [4, 4, 32], replicated, may hold values from 0.5 to 2
Outputs:
- solution: float32 [64, 12, 8192], P('scen', None, 'area')
- new_multipliers: float32 [64, 12, 1024], P('scen', None, 'area')
- consensus: float32 [12, 1024], P(None, 'area')
- spreads: float32 [4, 5], P('area')
The draws below stay inside these ranges and needn't reach their ends.
Inputs may be any that keep to these rules, and one draw needn't show every extreme that they name: `neighbour`: each entry names an area other than its row's own.
All inputs are finite; a program needn't handle non-finite values.
Results may differ from the reference program's by a relative error of at most 0.012.
Values may be sent and summed in bfloat16 or wider, within the bound.
A program may use at most 64 MiB of HBM per device.

```python
import math
import jax
import jax.numpy as jnp
from jax import lax

BUS = 2048
GEN = 256
PORTS = 128
KN = 4
TIE = 32
HOURS = 12
ITERS = 4
SCEN = 64
AREAS = 4


def draw_inverse(key, part):
    first_key, second_key = jax.random.split(jax.random.fold_in(key, 11))
    noise = jax.random.normal(first_key, (AREAS, BUS, BUS), jnp.float32) * (0.6 / math.sqrt(BUS))
    diagonal = jax.random.uniform(second_key, (AREAS, BUS), jnp.float32, 0.5, 1.5)
    matrix = noise + diagonal[:, :, None] * jnp.eye(BUS, dtype=jnp.float32)[None]
    return jnp.clip(matrix, -1.0, 2.0).reshape(AREAS * BUS, BUS).astype(jnp.bfloat16)


def draw_neighbour(key, part):
    offset = jax.random.randint(jax.random.fold_in(key, 23), (AREAS, KN), 1, AREAS)
    return ((jnp.arange(AREAS, dtype=jnp.int32)[:, None] + offset) % AREAS).astype(jnp.int32)


def set_ends(drawn, rng, low, high):
    longest = drawn.shape.index(max(drawn.shape))
    spots = []
    for shift in (0, 1):
        where = [jax.random.randint(jax.random.fold_in(rng, axis), (), 0, length) for axis, length in enumerate(drawn.shape)]
        where[longest] = (where[longest] + shift) % drawn.shape[longest]
        spots.append(tuple(where))
    return drawn.at[spots[0]].set(low).at[spots[1]].set(high)


def levels(stream_key, extent, shards, smallest, high):
    def one(dim, parts):
        heights = jax.random.uniform(jax.random.fold_in(jax.random.fold_in(stream_key, 6), dim), (parts,), jnp.float32, smallest / len(shards), high / len(shards))
        return jnp.repeat(jnp.exp(heights), extent[dim] // parts).reshape((-1,) + (1,) * (len(extent) - dim - 1))

    loudness = one(*shards[0])
    for cut in shards[1:]:
        loudness = loudness * one(*cut)
    return loudness


def scatter_about(own_key, shape, scale, bound, cuts=(), kind=jnp.bfloat16):
    result = scale * jax.random.normal(own_key, shape, jnp.float32)
    if cuts:
        result = result * levels(own_key, shape, cuts, -0.22, 0.18)
    return jnp.clip(result, -bound, bound).astype(kind)


def setup_inputs(seed: int = 0) -> dict:
    seeds = jax.random.split(jax.random.key(seed), 12)
    return {
        "load": scatter_about(seeds[0], (SCEN, HOURS, AREAS * BUS), 1.0, 6.0, ((0, 8), (2, 4)), jnp.float32),
        "start": scatter_about(seeds[1], (SCEN, HOURS, AREAS * BUS), 1.0, 6.0, ((0, 8), (2, 4)), jnp.float32),
        "multipliers": scatter_about(seeds[2], (SCEN, HOURS, AREAS * GEN), 0.5, 4.0, ((0, 8), (2, 4)), jnp.float32),
        "weights": jnp.clip(jnp.exp(math.log(4.0) - 2.7725887 * jax.random.uniform(seeds[3], (SCEN,), jnp.float32) ** levels(seeds[3], (SCEN,), ((0, 8),), -0.2, 0.2)), 0.25, 4.0),
        "penalty": jnp.clip(jnp.exp(math.log(3.0) - 2.3025851 * jax.random.uniform(seeds[4], (AREAS * GEN,), jnp.float32) ** levels(seeds[4], (AREAS * GEN,), ((0, 4),), -0.2, 0.2)), 0.3, 3.0),
        "inverse": draw_inverse(jax.random.fold_in(seeds[11], 71), 0),
        "ports": set_ends(jax.random.randint(seeds[6], (AREAS, PORTS), 0, BUS), jax.random.fold_in(seeds[6], 1), 0, BUS - 1).astype(jnp.int32),
        "neighbour": draw_neighbour(jax.random.fold_in(seeds[11], 71), 0),
        "remote_port": set_ends(jax.random.randint(seeds[8], (AREAS, KN, TIE), 0, PORTS), jax.random.fold_in(seeds[8], 1), 0, PORTS - 1).astype(jnp.int32),
        "local_bus": set_ends(jax.random.randint(seeds[9], (AREAS, KN, TIE), 0, BUS), jax.random.fold_in(seeds[9], 1), 0, BUS - 1).astype(jnp.int32),
        "susceptance": jnp.clip(jnp.exp(jax.random.uniform(seeds[10], (AREAS, KN, TIE), jnp.float32, math.log(0.5), math.log(2.0))), 0.5, 2.0),
    }


def scenario_mean(dispatch, weights):
    weight_sum = jnp.sum(weights)
    average = jnp.sum(weights[:, None, None, None] * dispatch, axis=0) / weight_sum
    deviation = dispatch - average[None]
    spread = jnp.sum(weights[:, None, None, None] * deviation * deviation, axis=(0, 1, 3)) / weight_sum / (HOURS * GEN)
    return average, spread


def reference(load, start, multipliers, weights, penalty, inverse, ports, neighbour, remote_port, local_bus, susceptance):
    row_count = SCEN * HOURS
    angles = start.reshape(row_count, AREAS, BUS)
    demand = load.reshape(row_count, AREAS, BUS)
    blocks = inverse.reshape(AREAS, BUS, BUS).astype(jnp.float32)
    duals = multipliers.reshape(SCEN, HOURS, AREAS, GEN)
    penalty_row = penalty.reshape(AREAS, GEN)
    area_index = jnp.broadcast_to(jnp.arange(AREAS, dtype=jnp.int32)[:, None, None], (AREAS, KN, TIE))
    average, spread = scenario_mean(angles[:, :, :GEN].reshape(SCEN, HOURS, AREAS, GEN), weights)
    spread_list = [spread]
    for iteration in range(ITERS):
        offered = jnp.take_along_axis(angles, ports[None, :, :], axis=2)
        offered = lax.optimization_barrier(offered.astype(jnp.bfloat16)).astype(jnp.float32)
        received = offered[:, neighbour[:, :, None], remote_port]
        inflow = jnp.zeros((row_count, AREAS, BUS), jnp.float32)
        inflow = inflow.at[:, area_index, local_bus].add(susceptance[None] * received)
        hedge = (penalty_row[None, None] * average[None] - duals).reshape(row_count, AREAS, GEN)
        right_side = demand + inflow
        right_side = right_side.at[:, :, :GEN].add(hedge)
        rounded = lax.optimization_barrier(right_side.astype(jnp.bfloat16)).astype(jnp.float32)
        angles = jnp.einsum("rab,abc->rac", rounded, blocks)
        dispatch = angles[:, :, :GEN].reshape(SCEN, HOURS, AREAS, GEN)
        average, spread = scenario_mean(dispatch, weights)
        duals = duals + penalty_row[None, None] * (dispatch - average[None])
        spread_list.append(spread)
    return (angles.reshape(SCEN, HOURS, AREAS * BUS), duals.reshape(SCEN, HOURS, AREAS * GEN), average.reshape(HOURS, AREAS * GEN), jnp.stack(spread_list, axis=1))
```

```python
import functools

import jax
import jax.numpy as jnp
from jax import lax
from jax.experimental import pallas as pl
from jax.experimental.pallas import tpu as pltpu
from jax.sharding import PartitionSpec as P

ITERS = 4
BLOCK = 256


def split(x):
    high = x.astype(jnp.bfloat16)
    low = (x - high.astype(jnp.float32)).astype(jnp.bfloat16)
    return high, low


def dot(a, b):
    return jnp.dot(a, b, preferred_element_type=jnp.float32)


def exact(a, b):
    return jnp.dot(a, b, precision=lax.Precision.HIGHEST, preferred_element_type=jnp.float32)


def iota(shape, axis):
    return lax.broadcasted_iota(jnp.int32, shape, axis)


def kernel(
    areas,
    groups,
    load_ref,
    start_ref,
    mult_ref,
    weight_ref,
    pen_ref,
    inv_ref,
    ports_ref,
    neigh_ref,
    rport_ref,
    lbus_ref,
    susc_ref,
    sol_ref,
    newm_ref,
    cons_ref,
    spread_ref,
    inv,
    left,
    start_b,
    full,
    h,
    pick,
    sel,
    acc,
    hsub,
    duals,
    ebuf,
    pbuf,
    dma_sem,
    esend,
    erecv,
    psend,
    precv,
):
    scen, hours, buses = load_ref.shape
    gens = mult_ref.shape[2]
    nports = ports_ref.shape[1]
    slots, ties = lbus_ref.shape[1:]
    width = slots * ties
    hp = pbuf.shape[2]
    rows = scen * hp
    blocks = buses // BLOCK
    area = lax.axis_index("area")
    group = lax.axis_index("scen")

    def fetch(j):
        cols = pl.ds(pl.multiple_of(j * BLOCK, BLOCK), BLOCK)
        return pltpu.make_async_copy(inv_ref.at[:, cols], inv.at[:, cols], dma_sem.at[j])

    for j in range(blocks):
        fetch(j).start()

    barrier = pltpu.get_barrier_semaphore()
    for o in range(1, areas):
        pl.semaphore_signal(
            barrier,
            inc=1,
            device_id={"area": lax.rem(area + o, areas)},
            device_id_type=pl.DeviceIdType.MESH,
        )
    for o in range(1, groups):
        pl.semaphore_signal(
            barrier,
            inc=1,
            device_id={"scen": lax.rem(group + o, groups)},
            device_id_type=pl.DeviceIdType.MESH,
        )

    def ecopy(i, o):
        return pltpu.make_async_remote_copy(
            src_ref=ebuf.at[i, area],
            dst_ref=ebuf.at[i, area],
            send_sem=esend.at[i, o],
            recv_sem=erecv.at[i, o],
            device_id={"area": lax.rem(area + o, areas)},
            device_id_type=pl.DeviceIdType.MESH,
        )

    def pcopy(i, o):
        return pltpu.make_async_remote_copy(
            src_ref=pbuf.at[i, group],
            dst_ref=pbuf.at[i, group],
            send_sem=psend.at[i, o],
            recv_sem=precv.at[i, o],
            device_id={"scen": lax.rem(group + o, groups)},
            device_id_type=pl.DeviceIdType.MESH,
        )

    row_id = iota((hp, gens), 0)
    weight_sum = weight_ref[0]
    for s in range(1, scen):
        weight_sum = weight_sum + weight_ref[s]

    def send_mean(i, x):
        total = jnp.zeros((hp, gens), jnp.float32)
        square = jnp.zeros((hp, gens), jnp.float32)
        for s in range(scen):
            part = x[s * hp : (s + 1) * hp, :]
            weighted = weight_ref[s] * part
            total = total + weighted
            square = square + weighted * part
        square = jnp.sum(square, axis=0, keepdims=True)
        total = jnp.where(row_id == hours, weight_sum, total)
        total = jnp.where(row_id == hours + 1, square, total)
        pbuf[i, group] = total
        for o in range(1, groups):
            pcopy(i, o).start()

    def get_mean(i):
        for o in range(1, groups):
            pcopy(i, o).wait_recv()
        total = pbuf[i, 0]
        for g in range(1, groups):
            total = total + pbuf[i, g]
        weights = total[hours : hours + 1, :]
        average = jnp.where(row_id < hours, total / weights, 0.0)
        squares = jnp.sum(total[hours + 1 : hours + 2, :])
        spread = (squares / jnp.max(weights) - jnp.sum(average * average)) / (hours * gens)
        return average, spread

    def send_ports(i, values):
        ebuf[i, area] = values.astype(jnp.bfloat16)
        for o in range(1, areas):
            ecopy(i, o).start()

    pick[...] = jnp.where(
        iota((buses, nports), 0) == ports_ref[pl.ds(area, 1), :], 1.0, 0.0
    ).astype(jnp.bfloat16)
    pad = jnp.zeros((hp - hours, buses), jnp.float32)
    for s in range(scen):
        start_b[s * hp : (s + 1) * hp, :] = jnp.concatenate(
            (start_ref[s], pad), axis=0
        ).astype(jnp.bfloat16)
    gpad = jnp.zeros((hp - hours, gens), jnp.float32)
    dispatch = jnp.concatenate(
        [
            piece
            for s in range(scen)
            for piece in (jnp.concatenate((start_ref[s, :, :gens], gpad), axis=0),)
        ],
        axis=0,
    )
    offered = dot(start_b[...], pick[...])
    pl.semaphore_wait(barrier, areas + groups - 2)
    send_ports(0, offered)
    send_mean(0, dispatch)

    def to_row(x):
        spread_out = exact(x, jnp.where(iota((ties, width), 1) % ties == iota((ties, width), 0), 1.0, 0.0))
        mine = iota((slots, width), 1) // ties == iota((slots, width), 0)
        return jnp.sum(jnp.where(mine, spread_out, 0.0), axis=0, keepdims=True)

    susc = to_row(susc_ref[area])
    rport = to_row(rport_ref[area].astype(jnp.float32))
    neigh = exact(
        neigh_ref[pl.ds(area, 1), :].astype(jnp.float32),
        jnp.where(iota((slots, width), 1) // ties == iota((slots, width), 0), 1.0, 0.0),
    )
    code = neigh * nports + rport
    sel[...] = jnp.where(
        iota((areas * nports, width), 0).astype(jnp.float32) == code, 1.0, 0.0
    ).astype(jnp.bfloat16)
    stretched = exact(
        jnp.where(iota((width, slots), 0) // ties == iota((width, slots), 1), 1.0, 0.0),
        lbus_ref[area].astype(jnp.float32),
    )
    mine = iota((width, ties), 0) % ties == iota((width, ties), 1)
    bus_col = jnp.sum(jnp.where(mine, stretched, 0.0), axis=1, keepdims=True)
    left[rows:, :] = jnp.where(
        iota((width, buses), 1).astype(jnp.float32) == bus_col, 1.0, 0.0
    ).astype(jnp.bfloat16)
    for s in range(scen):
        left[s * hp : (s + 1) * hp, :] = jnp.concatenate((load_ref[s], pad), axis=0).astype(
            jnp.bfloat16
        )
        duals[s * hp : (s + 1) * hp, :] = jnp.concatenate((mult_ref[s], gpad), axis=0)

    acc[...] = jnp.zeros_like(acc)

    def column_block(j, carry):
        fetch(j).wait()
        cols = pl.ds(pl.multiple_of(j * BLOCK, BLOCK), BLOCK)
        product = dot(left[...], inv[:, cols])
        own = product[:rows]
        full[:, cols] = own
        h[:width, cols] = product[rows:].astype(jnp.bfloat16)
        h[width:, cols] = inv[:gens, cols]
        high, low = split(own)
        stack = jnp.concatenate((high, low, h[:, cols]), axis=0)
        acc[...] += dot(stack, pick[cols, :])
        return carry

    lax.fori_loop(0, blocks, column_block, 0)

    base = jnp.concatenate((full[:, :gens], acc[:rows] + acc[rows : 2 * rows]), axis=1)
    hsub[...] = jnp.concatenate(
        (h[:, :gens], acc[2 * rows :].astype(jnp.bfloat16)), axis=1
    )
    pen = pen_ref[...]

    def gather(i, average):
        for o in range(1, areas):
            ecopy(i, o).wait_recv()
        received = dot(ebuf[i, 0], sel[:nports, :])
        for b in range(1, areas):
            received = received + dot(ebuf[i, b], sel[b * nports : (b + 1) * nports, :])
        hedge = jnp.concatenate([pen * average] * scen, axis=0) - duals[...]
        return jnp.concatenate((received * susc, hedge), axis=1)

    spreads = []
    average, spread = get_mean(0)
    spreads.append(spread)
    for i in range(ITERS):
        source = gather(i, average)
        high, low = split(source)
        update = base + dot(high, hsub[...]) + dot(low, hsub[...])
        if i < ITERS - 1:
            send_ports(i + 1, update[:, gens:])
        dispatch = update[:, :gens]
        send_mean(i + 1, dispatch)
        if i == ITERS - 1:
            for s in range(scen):
                sol_ref[s, :, :gens] = dispatch[s * hp : s * hp + hours]

            for j in range(gens // BLOCK, blocks):
                cols = slice(j * BLOCK, (j + 1) * BLOCK)
                out = full[:, cols] + dot(high, h[:, cols]) + dot(low, h[:, cols])
                for s in range(scen):
                    sol_ref[s, :, cols] = out[s * hp : s * hp + hours]
        average, spread = get_mean(i + 1)
        spreads.append(spread)
        duals[...] = duals[...] + pen * (dispatch - jnp.concatenate([average] * scen, axis=0))

    for s in range(scen):
        newm_ref[s] = duals[s * hp : s * hp + hours, :]
    cons_ref[...] = average[:hours]
    lane = iota(spread_ref.shape, 1)
    line = jnp.zeros(spread_ref.shape, jnp.float32)
    for i, spread in enumerate(spreads):
        line = jnp.where(lane == i, spread, line)
    spread_ref[...] = line

    for i in range(ITERS):
        for o in range(1, areas):
            ecopy(i, o).wait_send()
    for i in range(ITERS + 1):
        for o in range(1, groups):
            pcopy(i, o).wait_send()


def shards(areas, groups, load, start, multipliers, weights, penalty, inverse, *tables):
    scen, hours, buses = load.shape
    gens = multipliers.shape[2]
    ports, _, _, local_bus, _ = tables
    nports = ports.shape[1]
    width = local_bus.shape[1] * local_bus.shape[2]
    hp = -(-(hours + 2) // 16) * 16
    rows = scen * hp
    inner = width + gens
    bf, f32 = jnp.bfloat16, jnp.float32
    vmem = pl.BlockSpec(memory_space=pltpu.VMEM)
    dma = pltpu.SemaphoreType.DMA
    return pl.pallas_call(
        functools.partial(kernel, areas, groups),
        out_shape=(
            jax.ShapeDtypeStruct(load.shape, f32),
            jax.ShapeDtypeStruct(multipliers.shape, f32),
            jax.ShapeDtypeStruct((hours, gens), f32),
            jax.ShapeDtypeStruct((1, ITERS + 1), f32),
        ),
        in_specs=[
            vmem,
            vmem,
            vmem,
            pl.BlockSpec(memory_space=pltpu.SMEM),
            vmem,
            pl.BlockSpec(memory_space=pl.ANY),
        ]
        + [vmem] * 5,
        out_specs=(vmem,) * 4,
        scratch_shapes=[
            pltpu.VMEM((buses, buses), bf),
            pltpu.VMEM((rows + width, buses), bf),
            pltpu.VMEM((rows, buses), bf),
            pltpu.VMEM((rows, buses), f32),
            pltpu.VMEM((inner, buses), bf),
            pltpu.VMEM((buses, nports), bf),
            pltpu.VMEM((areas * nports, width), bf),
            pltpu.VMEM((2 * rows + inner, nports), f32),
            pltpu.VMEM((inner, gens + nports), bf),
            pltpu.VMEM((rows, gens), f32),
            pltpu.VMEM((ITERS, areas, rows, nports), bf),
            pltpu.VMEM((ITERS + 1, groups, hp, gens), f32),
            dma((buses // BLOCK,)),
            dma((ITERS, areas)),
            dma((ITERS, areas)),
            dma((ITERS + 1, groups)),
            dma((ITERS + 1, groups)),
        ],
        compiler_params=pltpu.CompilerParams(collective_id=0, has_side_effects=True),
        name="hedging",
    )(load, start, multipliers, weights, penalty.reshape(1, gens), inverse, *tables)


def solution(mesh):
    placed = (
        P("scen", None, "area"),
        P("scen", None, "area"),
        P("scen", None, "area"),
        P("scen"),
        P("area"),
        P("area", None),
        P(),
        P(),
        P(),
        P(),
        P(),
    )
    return jax.shard_map(
        functools.partial(shards, mesh.shape["area"], mesh.shape["scen"]),
        mesh=mesh,
        in_specs=placed,
        out_specs=(
            P("scen", None, "area"),
            P("scen", None, "area"),
            P(None, "area"),
            P("area", None),
        ),
        check_vma=False,
    )
```

```python
import functools

import jax
import jax.numpy as jnp
from jax import lax
from jax.experimental import pallas as pl
from jax.experimental.pallas import tpu as pltpu
from jax.sharding import PartitionSpec as P

ITERS = 4
BLOCK = 256


def split(x):
    high = x.astype(jnp.bfloat16)
    low = (x - high.astype(jnp.float32)).astype(jnp.bfloat16)
    return high, low


def dot(a, b):
    return jnp.dot(a, b, preferred_element_type=jnp.float32)


def exact(a, b):
    return jnp.dot(a, b, precision=lax.Precision.HIGHEST, preferred_element_type=jnp.float32)


def iota(shape, axis):
    return lax.broadcasted_iota(jnp.int32, shape, axis)


def kernel(
    areas,
    groups,
    load_ref,
    start_ref,
    mult_ref,
    weight_ref,
    pen_ref,
    inv_ref,
    ports_ref,
    neigh_ref,
    rport_ref,
    lbus_ref,
    susc_ref,
    sol_ref,
    newm_ref,
    cons_ref,
    spread_ref,
    inv,
    left,
    full,
    h,
    pick,
    sel,
    acc,
    hsub,
    duals,
    ebuf,
    pbuf,
    dma_sem,
    esend,
    erecv,
    psend,
    precv,
):
    rows, buses = load_ref.shape
    gens = mult_ref.shape[1]
    scen = weight_ref.shape[0]
    hours = rows // scen
    nports = ports_ref.shape[1]
    slots, ties = lbus_ref.shape[1:]
    width = slots * ties
    hp = pbuf.shape[2]
    blocks = buses // BLOCK
    area = lax.axis_index("area")
    group = lax.axis_index("scen")

    def fetch(j):
        cols = pl.ds(pl.multiple_of(j * BLOCK, BLOCK), BLOCK)
        return pltpu.make_async_copy(inv_ref.at[:, cols], inv.at[:, cols], dma_sem.at[j])

    for j in range(blocks):
        fetch(j).start()

    barrier = pltpu.get_barrier_semaphore()
    for o in range(1, areas):
        pl.semaphore_signal(
            barrier,
            inc=1,
            device_id={"area": lax.rem(area + o, areas)},
            device_id_type=pl.DeviceIdType.MESH,
        )
    for o in range(1, groups):
        pl.semaphore_signal(
            barrier,
            inc=1,
            device_id={"scen": lax.rem(group + o, groups)},
            device_id_type=pl.DeviceIdType.MESH,
        )

    def ecopy(i, o):
        return pltpu.make_async_remote_copy(
            src_ref=ebuf.at[i, area],
            dst_ref=ebuf.at[i, area],
            send_sem=esend.at[i, o],
            recv_sem=erecv.at[i, o],
            device_id={"area": lax.rem(area + o, areas)},
            device_id_type=pl.DeviceIdType.MESH,
        )

    def pcopy(i, o):
        return pltpu.make_async_remote_copy(
            src_ref=pbuf.at[i, group],
            dst_ref=pbuf.at[i, group],
            send_sem=psend.at[i, o],
            recv_sem=precv.at[i, o],
            device_id={"scen": lax.rem(group + o, groups)},
            device_id_type=pl.DeviceIdType.MESH,
        )

    seat = iota((scen, gens), 0)
    weights = jnp.zeros((scen, gens), jnp.float32)
    for s in range(scen):
        weights = jnp.where(seat == s, weight_ref[s], weights)
    weight_sum = jnp.sum(weights, axis=0, keepdims=True)

    def over_scenarios(x):
        return jnp.broadcast_to(x[:, None, :], (hours, scen, gens)).reshape(rows, gens)

    def send_mean(i, x):
        weighted = weights[None] * x.reshape(hours, scen, gens)
        square = jnp.sum(weighted * x.reshape(hours, scen, gens), axis=(0, 1))[None]
        pbuf[i, group, :hours, :] = jnp.sum(weighted, axis=1)
        pbuf[i, group, hours : hours + 1, :] = weight_sum
        pbuf[i, group, hours + 1 : hours + 2, :] = square
        if hp > hours + 2:
            pbuf[i, group, hours + 2 :, :] = jnp.zeros((hp - hours - 2, gens), jnp.float32)
        for o in range(1, groups):
            pcopy(i, o).start()

    def get_mean(i):
        for o in range(1, groups):
            pcopy(i, o).wait_recv()
        total = pbuf[i, 0]
        for g in range(1, groups):
            total = total + pbuf[i, g]
        everything = total[hours : hours + 1, :]
        average = total[:hours] / everything
        squares = jnp.sum(total[hours + 1 : hours + 2, :])
        spread = (squares / jnp.max(everything) - jnp.sum(average * average)) / (hours * gens)
        return average, spread

    def send_ports(i, values):
        ebuf[i, area] = values.astype(jnp.bfloat16)
        for o in range(1, areas):
            ecopy(i, o).start()

    pick[...] = jnp.where(
        iota((buses, nports), 0) == ports_ref[pl.ds(area, 1), :], 1.0, 0.0
    ).astype(jnp.bfloat16)
    start_b = start_ref[...].astype(jnp.bfloat16)
    dispatch = start_ref[:, :gens]
    offered = dot(start_b, pick[...])
    pl.semaphore_wait(barrier, areas + groups - 2)
    send_ports(0, offered)
    send_mean(0, dispatch)

    def to_row(x):
        spread_out = exact(x, jnp.where(iota((ties, width), 1) % ties == iota((ties, width), 0), 1.0, 0.0))
        mine = iota((slots, width), 1) // ties == iota((slots, width), 0)
        return jnp.sum(jnp.where(mine, spread_out, 0.0), axis=0, keepdims=True)

    susc = to_row(susc_ref[area])
    rport = to_row(rport_ref[area].astype(jnp.float32))
    neigh = exact(
        neigh_ref[pl.ds(area, 1), :].astype(jnp.float32),
        jnp.where(iota((slots, width), 1) // ties == iota((slots, width), 0), 1.0, 0.0),
    )
    code = neigh * nports + rport
    sel[...] = jnp.where(
        iota((areas * nports, width), 0).astype(jnp.float32) == code, 1.0, 0.0
    ).astype(jnp.bfloat16)
    stretched = exact(
        jnp.where(iota((width, slots), 0) // ties == iota((width, slots), 1), 1.0, 0.0),
        lbus_ref[area].astype(jnp.float32),
    )
    mine = iota((width, ties), 0) % ties == iota((width, ties), 1)
    bus_col = jnp.sum(jnp.where(mine, stretched, 0.0), axis=1, keepdims=True)
    left[rows:, :] = jnp.where(
        iota((width, buses), 1).astype(jnp.float32) == bus_col, 1.0, 0.0
    ).astype(jnp.bfloat16)
    left[:rows, :] = load_ref[...].astype(jnp.bfloat16)
    duals[...] = mult_ref[...]

    acc[...] = jnp.zeros_like(acc)

    def column_block(j, carry):
        fetch(j).wait()
        cols = pl.ds(pl.multiple_of(j * BLOCK, BLOCK), BLOCK)
        product = dot(left[...], inv[:, cols])
        own = product[:rows]
        full[:, cols] = own
        h[:width, cols] = product[rows:].astype(jnp.bfloat16)
        h[width:, cols] = inv[:gens, cols]
        high, low = split(own)
        stack = jnp.concatenate((high, low, h[:, cols]), axis=0)
        acc[...] += dot(stack, pick[cols, :])
        return carry

    lax.fori_loop(0, blocks, column_block, 0)

    base = jnp.concatenate((full[:, :gens], acc[:rows] + acc[rows : 2 * rows]), axis=1)
    hsub[...] = jnp.concatenate(
        (h[:, :gens], acc[2 * rows :].astype(jnp.bfloat16)), axis=1
    )
    pen = pen_ref[...]

    def gather(i, average):
        for o in range(1, areas):
            ecopy(i, o).wait_recv()
        received = dot(ebuf[i, 0], sel[:nports, :])
        for b in range(1, areas):
            received = received + dot(ebuf[i, b], sel[b * nports : (b + 1) * nports, :])
        hedge = over_scenarios(pen * average) - duals[...]
        return jnp.concatenate((received * susc, hedge), axis=1)

    spreads = []
    average, spread = get_mean(0)
    spreads.append(spread)
    for i in range(ITERS):
        source = gather(i, average)
        high, low = split(source)
        update = base + dot(high, hsub[...]) + dot(low, hsub[...])
        if i < ITERS - 1:
            send_ports(i + 1, update[:, gens:])
        dispatch = update[:, :gens]
        send_mean(i + 1, dispatch)
        if i == ITERS - 1:
            sol_ref[:, :gens] = dispatch
            for j in range(gens // BLOCK, blocks):
                cols = slice(j * BLOCK, (j + 1) * BLOCK)
                sol_ref[:, cols] = full[:, cols] + dot(high, h[:, cols]) + dot(low, h[:, cols])
        average, spread = get_mean(i + 1)
        spreads.append(spread)
        duals[...] = duals[...] + pen * (dispatch - over_scenarios(average))

    newm_ref[...] = duals[...]
    cons_ref[...] = average
    lane = iota(spread_ref.shape, 1)
    line = jnp.zeros(spread_ref.shape, jnp.float32)
    for i, spread in enumerate(spreads):
        line = jnp.where(lane == i, spread, line)
    spread_ref[...] = line

    for i in range(ITERS):
        for o in range(1, areas):
            ecopy(i, o).wait_send()
    for i in range(ITERS + 1):
        for o in range(1, groups):
            pcopy(i, o).wait_send()


def store(*refs):
    count = (len(refs) - 1) // 2
    copies = [
        pltpu.make_async_copy(refs[i], refs[count + i], refs[-1].at[i]) for i in range(count)
    ]
    for copy in copies:
        copy.start()
    for copy in copies:
        copy.wait()


def shards(areas, groups, load, start, multipliers, weights, penalty, inverse, *tables):
    scen, hours, buses = load.shape
    gens = multipliers.shape[2]
    rows = scen * hours
    load, start, multipliers = (
        x.transpose(1, 0, 2).reshape(rows, -1) for x in (load, start, multipliers)
    )
    ports, _, _, local_bus, _ = tables
    nports = ports.shape[1]
    width = local_bus.shape[1] * local_bus.shape[2]
    hp = -(-(hours + 2) // 8) * 8
    inner = width + gens
    bf, f32 = jnp.bfloat16, jnp.float32
    vmem = pl.BlockSpec(memory_space=pltpu.VMEM)
    dma = pltpu.SemaphoreType.DMA
    results = pl.pallas_call(
        functools.partial(kernel, areas, groups),
        out_shape=(
            jax.ShapeDtypeStruct(load.shape, f32),
            jax.ShapeDtypeStruct(multipliers.shape, f32),
            jax.ShapeDtypeStruct((hours, gens), f32),
            jax.ShapeDtypeStruct((1, ITERS + 1), f32),
        ),
        in_specs=[
            vmem,
            vmem,
            vmem,
            pl.BlockSpec(memory_space=pltpu.SMEM),
            vmem,
            pl.BlockSpec(memory_space=pl.ANY),
        ]
        + [vmem] * 5,
        out_specs=(vmem,) * 4,
        scratch_shapes=[
            pltpu.VMEM((buses, buses), bf),
            pltpu.VMEM((rows + width, buses), bf),
            pltpu.VMEM((rows, buses), f32),
            pltpu.VMEM((inner, buses), bf),
            pltpu.VMEM((buses, nports), bf),
            pltpu.VMEM((areas * nports, width), bf),
            pltpu.VMEM((2 * rows + inner, nports), f32),
            pltpu.VMEM((inner, gens + nports), bf),
            pltpu.VMEM((rows, gens), f32),
            pltpu.VMEM((ITERS, areas, rows, nports), bf),
            pltpu.VMEM((ITERS + 1, groups, hp, gens), f32),
            dma((buses // BLOCK,)),
            dma((ITERS, areas)),
            dma((ITERS, areas)),
            dma((ITERS + 1, groups)),
            dma((ITERS + 1, groups)),
        ],
        compiler_params=pltpu.CompilerParams(collective_id=0, has_side_effects=True),
        name="hedging",
    )(load, start, multipliers, weights, penalty.reshape(1, gens), inverse, *tables)
    solved, duals, average, spread = pl.pallas_call(
        store,
        out_shape=tuple(jax.ShapeDtypeStruct(x.shape, x.dtype) for x in results),
        in_specs=[vmem] * 4,
        out_specs=(pl.BlockSpec(memory_space=pl.ANY),) * 4,
        scratch_shapes=[dma((4,))],
        name="store",
    )(*results)
    solved, duals = (
        x.reshape(hours, scen, -1).transpose(1, 0, 2) for x in (solved, duals)
    )
    return solved, duals, average, spread


def solution(mesh):
    placed = (
        P("scen", None, "area"),
        P("scen", None, "area"),
        P("scen", None, "area"),
        P("scen"),
        P("area"),
        P("area", None),
        P(),
        P(),
        P(),
        P(),
        P(),
    )
    return jax.shard_map(
        functools.partial(shards, mesh.shape["area"], mesh.shape["scen"]),
        mesh=mesh,
        in_specs=placed,
        out_specs=(
            P("scen", None, "area"),
            P("scen", None, "area"),
            P(None, "area"),
            P("area", None),
        ),
        check_vma=False,
    )
```

```python
import functools

import jax
import jax.numpy as jnp
from jax import lax
from jax.experimental import pallas as pl
from jax.experimental.pallas import tpu as pltpu
from jax.sharding import PartitionSpec as P

ITERS = 4
BLOCK = 256


def split(x):
    high = x.astype(jnp.bfloat16)
    low = (x - high.astype(jnp.float32)).astype(jnp.bfloat16)
    return high, low


def dot(a, b):
    return jnp.dot(a, b, preferred_element_type=jnp.float32)


def exact(a, b):
    return jnp.dot(a, b, precision=lax.Precision.HIGHEST, preferred_element_type=jnp.float32)


def iota(shape, axis):
    return lax.broadcasted_iota(jnp.int32, shape, axis)


def kernel(
    areas,
    groups,
    load_hbm,
    start_hbm,
    mult_ref,
    weight_ref,
    pen_ref,
    inv_ref,
    ports_ref,
    neigh_ref,
    rport_ref,
    lbus_ref,
    susc_ref,
    sol_ref,
    newm_ref,
    cons_ref,
    spread_ref,
    inv,
    load_ref,
    start_ref,
    left,
    full,
    h,
    pick,
    sel,
    acc,
    hsub,
    duals,
    ebuf,
    pbuf,
    qbuf,
    dma_sem,
    in_sem,
    esend,
    erecv,
    psend,
    precv,
    qsend,
    qrecv,
):
    rows, buses = load_ref.shape
    gens = mult_ref.shape[1]
    scen = weight_ref.shape[0]
    hours = rows // scen
    nports = ports_ref.shape[1]
    slots, ties = lbus_ref.shape[1:]
    width = slots * ties
    hp = pbuf.shape[2]
    blocks = buses // BLOCK
    area = lax.axis_index("area")
    group = lax.axis_index("scen")

    def fetch(j):
        cols = pl.ds(pl.multiple_of(j * BLOCK, BLOCK), BLOCK)
        return pltpu.make_async_copy(inv_ref.at[:, cols], inv.at[:, cols], dma_sem.at[j])

    load_in = pltpu.make_async_copy(load_hbm, load_ref, in_sem.at[0])
    start_in = pltpu.make_async_copy(start_hbm, start_ref, in_sem.at[1])
    start_in.start()
    load_in.start()
    for j in range(blocks):
        fetch(j).start()

    barrier = pltpu.get_barrier_semaphore()
    for o in range(1, areas):
        pl.semaphore_signal(
            barrier,
            inc=1,
            device_id={"area": lax.rem(area + o, areas)},
            device_id_type=pl.DeviceIdType.MESH,
        )
    for o in range(1, groups):
        pl.semaphore_signal(
            barrier,
            inc=1,
            device_id={"scen": lax.rem(group + o, groups)},
            device_id_type=pl.DeviceIdType.MESH,
        )

    def ecopy(i, o):
        first = rows if i == ITERS else 0
        count = (rows if i == 0 else rows + hp) - first
        part = ebuf.at[i, area, pl.ds(first, count)]
        return pltpu.make_async_remote_copy(
            src_ref=part,
            dst_ref=part,
            send_sem=esend.at[i, o],
            recv_sem=erecv.at[i, o],
            device_id={"area": lax.rem(area + o, areas)},
            device_id_type=pl.DeviceIdType.MESH,
        )

    def pcopy(i, o):
        return pltpu.make_async_remote_copy(
            src_ref=pbuf.at[i, group],
            dst_ref=pbuf.at[i, group],
            send_sem=psend.at[i, o],
            recv_sem=precv.at[i, o],
            device_id={"scen": lax.rem(group + o, groups)},
            device_id_type=pl.DeviceIdType.MESH,
        )

    def qcopy(o):
        return pltpu.make_async_remote_copy(
            src_ref=qbuf.at[group],
            dst_ref=qbuf.at[group],
            send_sem=qsend.at[o],
            recv_sem=qrecv.at[o],
            device_id={"scen": lax.rem(group + o, groups)},
            device_id_type=pl.DeviceIdType.MESH,
        )

    inside = gens + nports
    seat = iota((scen, inside), 0)
    weights = jnp.zeros((scen, inside), jnp.float32)
    for s in range(scen):
        weights = jnp.where(seat == s, weight_ref[s], weights)
    weight_sum = jnp.sum(weights, axis=0, keepdims=True)
    row_id = iota((hp, inside), 0)

    def over_scenarios(x):
        return jnp.broadcast_to(x[:hours, None, :], (hours, scen, gens)).reshape(rows, gens)

    def send_sums(i, x):
        sums = jnp.sum(weights[None] * x.reshape(hours, scen, inside), axis=1)
        sums = jnp.concatenate((sums, jnp.zeros((hp - hours, inside), jnp.float32)), axis=0)
        if i == 0:
            rest = weight_sum
            for r in range(hours, hours + 3):
                piece = rest.astype(jnp.bfloat16).astype(jnp.float32)
                sums = jnp.where(row_id == r, piece, sums)
                rest = rest - piece
        pbuf[i, group] = sums.astype(jnp.bfloat16)
        for o in range(1, groups):
            pcopy(i, o).start()

    def get_sums(i):
        for o in range(1, groups):
            pcopy(i, o).wait_recv()
        total = pbuf[i, 0].astype(jnp.float32)
        for g in range(1, groups):
            total = total + pbuf[i, g].astype(jnp.float32)
        return total

    def squares(x, center):
        off = x - over_scenarios(center)
        off = off.reshape(hours, scen, gens)
        return jnp.sum(weights[None, :, :gens] * off * off)

    def send_exchange(i):
        for o in range(1, areas):
            ecopy(i, o).start()

    pick[...] = jnp.where(
        iota((buses, nports), 0) == ports_ref[pl.ds(area, 1), :], 1.0, 0.0
    ).astype(jnp.bfloat16)
    start_in.wait()
    start_b = start_ref[...].astype(jnp.bfloat16)
    dispatch = start_ref[:, :gens]
    offered = dot(start_b, pick[...])
    pl.semaphore_wait(barrier, areas + groups - 2)
    ebuf[0, area, :rows, :] = offered.astype(jnp.bfloat16)
    send_exchange(0)
    send_sums(0, jnp.concatenate((dispatch, offered), axis=1))

    def to_row(x):
        spread_out = exact(x, jnp.where(iota((ties, width), 1) % ties == iota((ties, width), 0), 1.0, 0.0))
        mine = iota((slots, width), 1) // ties == iota((slots, width), 0)
        return jnp.sum(jnp.where(mine, spread_out, 0.0), axis=0, keepdims=True)

    susc = to_row(susc_ref[area])
    rport = to_row(rport_ref[area].astype(jnp.float32))
    neigh = exact(
        neigh_ref[pl.ds(area, 1), :].astype(jnp.float32),
        jnp.where(iota((slots, width), 1) // ties == iota((slots, width), 0), 1.0, 0.0),
    )
    code = neigh * nports + rport
    sel[...] = jnp.where(
        iota((areas * nports, width), 0).astype(jnp.float32) == code, 1.0, 0.0
    ).astype(jnp.bfloat16)
    stretched = exact(
        jnp.where(iota((width, slots), 0) // ties == iota((width, slots), 1), 1.0, 0.0),
        lbus_ref[area].astype(jnp.float32),
    )
    mine = iota((width, ties), 0) % ties == iota((width, ties), 1)
    bus_col = jnp.sum(jnp.where(mine, stretched, 0.0), axis=1, keepdims=True)
    left[rows:, :] = jnp.where(
        iota((width, buses), 1).astype(jnp.float32) == bus_col, 1.0, 0.0
    ).astype(jnp.bfloat16)
    load_in.wait()
    left[:rows, :] = load_ref[...].astype(jnp.bfloat16)

    acc[...] = jnp.zeros_like(acc)

    def column_block(j, carry):
        fetch(j).wait()
        cols = pl.ds(pl.multiple_of(j * BLOCK, BLOCK), BLOCK)
        product = dot(left[...], inv[:, cols])
        own = product[:rows]
        full[:, cols] = own
        h[:width, cols] = product[rows:].astype(jnp.bfloat16)
        h[width:, cols] = inv[:gens, cols]
        high, low = split(own)
        stack = jnp.concatenate((high, low, h[:, cols]), axis=0)
        acc[...] += dot(stack, pick[cols, :])
        return carry

    lax.fori_loop(0, blocks, column_block, 0)

    base = jnp.concatenate((full[:, :gens], acc[:rows] + acc[rows : 2 * rows]), axis=1)
    hsub[...] = jnp.concatenate(
        (h[:, :gens], acc[2 * rows :].astype(jnp.bfloat16)), axis=1
    )
    pen = pen_ref[...]

    def apply(source):
        high, low = split(source)
        return dot(high, hsub[...]) + dot(low, hsub[...])

    high, low = split(mult_ref[...])
    still = base - dot(high, hsub[width:, :]) - dot(low, hsub[width:, :])
    send_sums(1, still)
    total = get_sums(0)
    everything = total[hours : hours + 1, :]
    for r in range(hours + 1, hours + 3):
        everything = everything + total[r : r + 1, :]
    mean = jnp.where(row_id < hours, total / everything, 0.0)
    duals[...] = mult_ref[...]
    numerators = []
    for i in range(ITERS):
        average = mean[:, :gens]
        for o in range(1, areas):
            ecopy(i, o).wait_recv()
        top = rows if i == 0 else rows + hp
        received = dot(ebuf[i, 0, :top, :], sel[:nports, :])
        for b in range(1, areas):
            received = received + dot(
                ebuf[i, b, :top, :], sel[b * nports : (b + 1) * nports, :]
            )
        received = received * susc
        if i > 0:
            if i == 1:
                still_mean = get_sums(1) / everything
            source = jnp.concatenate((received[rows:], pen * average), axis=1)
            mean = still_mean + apply(source)
            average = mean[:, :gens]
            duals[...] = duals[...] + pen * (dispatch - over_scenarios(average))
        if i == ITERS - 1:
            ebuf[ITERS, area, rows:, :] = mean[:, gens:].astype(jnp.bfloat16)
            send_exchange(ITERS)
        hedge = over_scenarios(pen * average) - duals[...]
        source = jnp.concatenate((received[:rows], hedge), axis=1)
        update = base + apply(source)
        previous, dispatch = dispatch, update[:, :gens]
        if i < ITERS - 1:
            ebuf[i + 1, area, :rows, :] = update[:, gens:].astype(jnp.bfloat16)
            ebuf[i + 1, area, rows:, :] = mean[:, gens:].astype(jnp.bfloat16)
            send_exchange(i + 1)
        numerators.append(squares(previous, average))

    numerators.append(squares(dispatch, average))
    lane = iota(qbuf.shape[1:], 1)
    line = jnp.zeros(qbuf.shape[1:], jnp.float32)
    for i, value in enumerate(numerators):
        line = jnp.where(lane == i, value, line)
    qbuf[group] = line
    for o in range(1, groups):
        qcopy(o).start()

    high, low = split(source)
    sol_ref[:, :gens] = dispatch
    for j in range(gens // BLOCK, blocks):
        cols = slice(j * BLOCK, (j + 1) * BLOCK)
        sol_ref[:, cols] = full[:, cols] + dot(high, h[:, cols]) + dot(low, h[:, cols])

    for o in range(1, areas):
        ecopy(ITERS, o).wait_recv()
    received = dot(ebuf[ITERS, 0, rows:, :], sel[:nports, :])
    for b in range(1, areas):
        received = received + dot(
            ebuf[ITERS, b, rows:, :], sel[b * nports : (b + 1) * nports, :]
        )
    source = jnp.concatenate((received * susc, pen * average), axis=1)
    last = (still_mean + apply(source))[:, :gens]
    newm_ref[...] = duals[...] + pen * (dispatch - over_scenarios(last))
    cons_ref[...] = last[:hours]
    for o in range(1, groups):
        qcopy(o).wait_recv()
    line = qbuf[0]
    for g in range(1, groups):
        line = line + qbuf[g]
    step = (last - average)[:hours]
    line = line[:1, : ITERS + 1] / everything[:, : ITERS + 1]
    line = jnp.where(iota(line.shape, 1) == ITERS, line - jnp.sum(step * step), line)
    spread_ref[...] = line / (hours * gens)

    for i in range(ITERS + 1):
        for o in range(1, areas):
            ecopy(i, o).wait_send()
    for o in range(1, groups):
        for i in range(2):
            pcopy(i, o).wait_send()
        qcopy(o).wait_send()


def store(*refs):
    count = (len(refs) - 1) // 2
    copies = [
        pltpu.make_async_copy(refs[i], refs[count + i], refs[-1].at[i]) for i in range(count)
    ]
    for copy in copies:
        copy.start()
    for copy in copies:
        copy.wait()


def shards(areas, groups, load, start, multipliers, weights, penalty, inverse, *tables):
    scen, hours, buses = load.shape
    gens = multipliers.shape[2]
    rows = scen * hours
    load, start, multipliers = (
        x.transpose(1, 0, 2).reshape(rows, -1) for x in (load, start, multipliers)
    )
    ports, _, _, local_bus, _ = tables
    nports = ports.shape[1]
    width = local_bus.shape[1] * local_bus.shape[2]
    hp = -(-(hours + 3) // 16) * 16
    inner = width + gens
    bf, f32 = jnp.bfloat16, jnp.float32
    vmem = pl.BlockSpec(memory_space=pltpu.VMEM)
    dma = pltpu.SemaphoreType.DMA
    results = pl.pallas_call(
        functools.partial(kernel, areas, groups),
        out_shape=(
            jax.ShapeDtypeStruct(load.shape, f32),
            jax.ShapeDtypeStruct(multipliers.shape, f32),
            jax.ShapeDtypeStruct((hours, gens), f32),
            jax.ShapeDtypeStruct((1, ITERS + 1), f32),
        ),
        in_specs=[
            pl.BlockSpec(memory_space=pl.ANY),
            pl.BlockSpec(memory_space=pl.ANY),
            vmem,
            pl.BlockSpec(memory_space=pltpu.SMEM),
            vmem,
            pl.BlockSpec(memory_space=pl.ANY),
        ]
        + [vmem] * 5,
        out_specs=(vmem,) * 4,
        scratch_shapes=[
            pltpu.VMEM((buses, buses), bf),
            pltpu.VMEM((rows, buses), f32),
            pltpu.VMEM((rows, buses), f32),
            pltpu.VMEM((rows + width, buses), bf),
            pltpu.VMEM((rows, buses), f32),
            pltpu.VMEM((inner, buses), bf),
            pltpu.VMEM((buses, nports), bf),
            pltpu.VMEM((areas * nports, width), bf),
            pltpu.VMEM((2 * rows + inner, nports), f32),
            pltpu.VMEM((inner, gens + nports), bf),
            pltpu.VMEM((rows, gens), f32),
            pltpu.VMEM((ITERS + 1, areas, rows + hp, nports), bf),
            pltpu.VMEM((2, groups, hp, gens + nports), bf),
            pltpu.VMEM((groups, 8, 128), f32),
            dma((buses // BLOCK,)),
            dma((2,)),
            dma((ITERS + 1, areas)),
            dma((ITERS + 1, areas)),
            dma((2, groups)),
            dma((2, groups)),
            dma((groups,)),
            dma((groups,)),
        ],
        compiler_params=pltpu.CompilerParams(collective_id=0, has_side_effects=True),
        name="hedging",
    )(load, start, multipliers, weights, penalty.reshape(1, gens), inverse, *tables)
    solved, duals, average, spread = pl.pallas_call(
        store,
        out_shape=tuple(jax.ShapeDtypeStruct(x.shape, x.dtype) for x in results),
        in_specs=[vmem] * 4,
        out_specs=(pl.BlockSpec(memory_space=pl.ANY),) * 4,
        scratch_shapes=[dma((4,))],
        name="store",
    )(*results)
    solved, duals = (
        x.reshape(hours, scen, -1).transpose(1, 0, 2) for x in (solved, duals)
    )
    return solved, duals, average, spread


def solution(mesh):
    placed = (
        P("scen", None, "area"),
        P("scen", None, "area"),
        P("scen", None, "area"),
        P("scen"),
        P("area"),
        P("area", None),
        P(),
        P(),
        P(),
        P(),
        P(),
    )
    return jax.shard_map(
        functools.partial(shards, mesh.shape["area"], mesh.shape["scen"]),
        mesh=mesh,
        in_specs=placed,
        out_specs=(
            P("scen", None, "area"),
            P("scen", None, "area"),
            P(None, "area"),
            P("area", None),
        ),
        check_vma=False,
    )
```

```python
import functools

import jax
import jax.numpy as jnp
from jax import lax
from jax.experimental import pallas as pl
from jax.experimental.pallas import tpu as pltpu
from jax.sharding import PartitionSpec as P

ITERS = 4
BLOCK = 256


def split(x):
    high = x.astype(jnp.bfloat16)
    low = (x - high.astype(jnp.float32)).astype(jnp.bfloat16)
    return high, low


def dot(a, b):
    return jnp.dot(a, b, preferred_element_type=jnp.float32)


def exact(a, b):
    total = jnp.zeros((a.shape[0], b.shape[1]), jnp.float32)
    rest, other, first = (b, a, False) if a.shape[1] == b.shape[0] and a.shape[0] > b.shape[1] else (a, b, True)
    for _ in range(3):
        piece = rest.astype(jnp.bfloat16)
        rest = rest - piece.astype(jnp.float32)
        total = total + (dot(piece, other.astype(jnp.bfloat16)) if first else dot(other.astype(jnp.bfloat16), piece))
    return total


def iota(shape, axis):
    return lax.broadcasted_iota(jnp.int32, shape, axis)


def kernel(
    areas,
    groups,
    load_hbm,
    start_hbm,
    mult_ref,
    weight_ref,
    pen_ref,
    inv_ref,
    ports_ref,
    neigh_ref,
    rport_ref,
    lbus_ref,
    susc_ref,
    sol_hbm,
    newm_ref,
    cons_ref,
    spread_ref,
    inv,
    sol_ref,
    load_ref,
    start_ref,
    left,
    full,
    h,
    pick,
    sel,
    acc,
    hsub,
    duals,
    ebuf,
    pbuf,
    qbuf,
    dma_sem,
    out_sem,
    in_sem,
    esend,
    erecv,
    psend,
    precv,
    qsend,
    qrecv,
):
    rows, buses = load_ref.shape
    gens = mult_ref.shape[1]
    scen = weight_ref.shape[0]
    hours = rows // scen
    nports = ports_ref.shape[1]
    slots, ties = lbus_ref.shape[1:]
    width = slots * ties
    hp = pbuf.shape[2]
    blocks = buses // BLOCK
    area = lax.axis_index("area")
    group = lax.axis_index("scen")

    def fetch(j):
        cols = pl.ds(pl.multiple_of(j * BLOCK, BLOCK), BLOCK)
        return pltpu.make_async_copy(inv_ref.at[:, cols], inv.at[:, cols], dma_sem.at[j])

    load_in = pltpu.make_async_copy(load_hbm, load_ref, in_sem.at[0])
    start_in = pltpu.make_async_copy(start_hbm, start_ref, in_sem.at[1])
    start_in.start()
    load_in.start()
    for j in range(blocks):
        fetch(j).start()

    barrier = pltpu.get_barrier_semaphore()
    for o in range(1, areas):
        pl.semaphore_signal(
            barrier,
            inc=1,
            device_id={"area": lax.rem(area + o, areas)},
            device_id_type=pl.DeviceIdType.MESH,
        )
    for o in range(1, groups):
        pl.semaphore_signal(
            barrier,
            inc=1,
            device_id={"scen": lax.rem(group + o, groups)},
            device_id_type=pl.DeviceIdType.MESH,
        )

    def ecopy(i, o):
        first = rows if i == ITERS else 0
        count = (rows if i == 0 else rows + hp) - first
        part = ebuf.at[i, area, pl.ds(first, count)]
        return pltpu.make_async_remote_copy(
            src_ref=part,
            dst_ref=part,
            send_sem=esend.at[i, o],
            recv_sem=erecv.at[i, o],
            device_id={"area": lax.rem(area + o, areas)},
            device_id_type=pl.DeviceIdType.MESH,
        )

    def pcopy(i, o):
        return pltpu.make_async_remote_copy(
            src_ref=pbuf.at[i, group],
            dst_ref=pbuf.at[i, group],
            send_sem=psend.at[i, o],
            recv_sem=precv.at[i, o],
            device_id={"scen": lax.rem(group + o, groups)},
            device_id_type=pl.DeviceIdType.MESH,
        )

    def qcopy(o):
        return pltpu.make_async_remote_copy(
            src_ref=qbuf.at[group],
            dst_ref=qbuf.at[group],
            send_sem=qsend.at[o],
            recv_sem=qrecv.at[o],
            device_id={"scen": lax.rem(group + o, groups)},
            device_id_type=pl.DeviceIdType.MESH,
        )

    inside = gens + nports
    seat = iota((scen, inside), 0)
    weights = jnp.zeros((scen, inside), jnp.float32)
    for s in range(scen):
        weights = jnp.where(seat == s, weight_ref[s], weights)
    weight_sum = jnp.sum(weights, axis=0, keepdims=True)
    row_id = iota((hp, inside), 0)

    def over_scenarios(x):
        return jnp.broadcast_to(x[:hours, None, :], (hours, scen, x.shape[1])).reshape(rows, x.shape[1])

    def send_sums(i, x):
        sums = jnp.sum(weights[None] * x.reshape(hours, scen, inside), axis=1)
        sums = jnp.concatenate((sums, jnp.zeros((hp - hours, inside), jnp.float32)), axis=0)
        if i == 0:
            rest = weight_sum
            for r in range(hours, hours + 3):
                piece = rest.astype(jnp.bfloat16).astype(jnp.float32)
                sums = jnp.where(row_id == r, piece, sums)
                rest = rest - piece
        pbuf[i, group] = sums.astype(jnp.bfloat16)
        for o in range(1, groups):
            pcopy(i, o).start()

    def get_sums(i):
        for o in range(1, groups):
            pcopy(i, o).wait_recv()
        total = pbuf[i, 0].astype(jnp.float32)
        for g in range(1, groups):
            total = total + pbuf[i, g].astype(jnp.float32)
        return total

    def squares(x, center):
        off = x - over_scenarios(center)
        off = off.reshape(hours, scen, gens)
        return jnp.sum(weights[None, :, :gens] * off * off)

    def send_exchange(i):
        for o in range(1, areas):
            ecopy(i, o).start()

    pick[...] = jnp.where(
        iota((buses, nports), 0) == ports_ref[pl.ds(area, 1), :], 1.0, 0.0
    ).astype(jnp.bfloat16)
    start_in.wait()
    start_b = start_ref[...].astype(jnp.bfloat16)
    dispatch = start_ref[:, :gens]
    offered = dot(start_b, pick[...])
    pl.semaphore_wait(barrier, areas + groups - 2)
    ebuf[0, area, :rows, :] = offered.astype(jnp.bfloat16)
    send_exchange(0)
    send_sums(0, jnp.concatenate((dispatch, offered), axis=1))

    def to_row(x):
        spread_out = exact(x, jnp.where(iota((ties, width), 1) % ties == iota((ties, width), 0), 1.0, 0.0))
        mine = iota((slots, width), 1) // ties == iota((slots, width), 0)
        return jnp.sum(jnp.where(mine, spread_out, 0.0), axis=0, keepdims=True)

    susc = to_row(susc_ref[area])
    rport = to_row(rport_ref[area].astype(jnp.float32))
    neigh = exact(
        neigh_ref[pl.ds(area, 1), :].astype(jnp.float32),
        jnp.where(iota((slots, width), 1) // ties == iota((slots, width), 0), 1.0, 0.0),
    )
    code = neigh * nports + rport
    sel[...] = jnp.where(
        iota((areas * nports, width), 0).astype(jnp.float32) == code, 1.0, 0.0
    ).astype(jnp.bfloat16)
    stretched = exact(
        jnp.where(iota((width, slots), 0) // ties == iota((width, slots), 1), 1.0, 0.0),
        lbus_ref[area].astype(jnp.float32),
    )
    mine = iota((width, ties), 0) % ties == iota((width, ties), 1)
    bus_col = jnp.sum(jnp.where(mine, stretched, 0.0), axis=1, keepdims=True)
    left[rows:, :] = jnp.where(
        iota((width, buses), 1).astype(jnp.float32) == bus_col, 1.0, 0.0
    ).astype(jnp.bfloat16)
    load_in.wait()
    left[:rows, :] = load_ref[...].astype(jnp.bfloat16)

    acc[...] = jnp.zeros_like(acc)

    def column_block(j, carry):
        fetch(j).wait()
        cols = pl.ds(pl.multiple_of(j * BLOCK, BLOCK), BLOCK)
        product = dot(left[...], inv[:, cols])
        own = product[:rows]
        full[:, cols] = own
        h[:width, cols] = product[rows:].astype(jnp.bfloat16)
        h[width:, cols] = inv[:gens, cols]
        high, low = split(own)
        stack = jnp.concatenate((high, low, h[:, cols]), axis=0)
        acc[...] += dot(stack, pick[cols, :])
        return carry

    lax.fori_loop(0, blocks, column_block, 0)

    base = jnp.concatenate((full[:, :gens], acc[:rows] + acc[rows : 2 * rows]), axis=1)
    hsub[...] = jnp.concatenate(
        (h[:, :gens], acc[2 * rows :].astype(jnp.bfloat16)), axis=1
    )
    pen = pen_ref[...]

    def through(source, first, count):
        high, low = split(source)
        part = hsub[first : first + count, :]
        return dot(high, part) + dot(low, part)

    def arrived(i, first, count):
        for o in range(1, areas):
            ecopy(i, o).wait_recv()
        received = dot(ebuf[i, 0, first : first + count, :], sel[:nports, :])
        for b in range(1, areas):
            received = received + dot(
                ebuf[i, b, first : first + count, :], sel[b * nports : (b + 1) * nports, :]
            )
        received = received * susc
        return received, dot(received.astype(jnp.bfloat16), hsub[:width, :])

    still = base - through(mult_ref[...], width, gens)
    send_sums(1, still)
    total = get_sums(0)
    everything = total[hours : hours + 1, :]
    for r in range(hours + 1, hours + 3):
        everything = everything + total[r : r + 1, :]
    mean = jnp.where(row_id < hours, total / everything, 0.0)
    duals[...] = mult_ref[...]
    numerators = []
    before = still
    for i in range(ITERS):
        received, added = arrived(i, 0, rows if i == 0 else rows + hp)
        if i > 0:
            if i == 1:
                still_mean = get_sums(1) / everything
            mean = still_mean + pull + added[rows:]
        average = mean[:, :gens]
        if i == ITERS - 1:
            ebuf[ITERS, area, rows:, :] = mean[:, gens:].astype(jnp.bfloat16)
            send_exchange(ITERS)
        pull = through(pen * average, width, gens)
        update = before + added[:rows] + over_scenarios(pull if i == 0 else pull + pull)
        previous, dispatch = dispatch, update[:, :gens]
        if i < ITERS - 1:
            ebuf[i + 1, area, :rows, :] = update[:, gens:].astype(jnp.bfloat16)
            ebuf[i + 1, area, rows:, :] = mean[:, gens:].astype(jnp.bfloat16)
            send_exchange(i + 1)
        if i > 0:
            duals[...] = duals[...] + pen * (previous - over_scenarios(average))
        numerators.append(squares(previous, average))
        if i < ITERS - 1:
            before = base - through(duals[...] + pen * dispatch, width, gens)

    numerators.append(squares(dispatch, average))
    lane = iota(qbuf.shape[1:], 1)
    line = jnp.zeros(qbuf.shape[1:], jnp.float32)
    for i, value in enumerate(numerators):
        line = jnp.where(lane == i, value, line)
    qbuf[group] = line
    for o in range(1, groups):
        qcopy(o).start()

    hedge = over_scenarios(pen * average) - duals[...]
    high = jnp.concatenate((received[:rows], hedge), axis=1).astype(jnp.bfloat16)
    sol_ref[:, :gens] = dispatch
    for j in range(gens // BLOCK, blocks):
        cols = slice(j * BLOCK, (j + 1) * BLOCK)
        sol_ref[:, cols] = full[:, cols] + dot(high, h[:, cols])

    solved = pltpu.make_async_copy(sol_ref, sol_hbm, out_sem)
    solved.start()

    _, added = arrived(ITERS, rows, hp)
    last = (still_mean + pull + added)[:, :gens]
    newm_ref[...] = duals[...] + pen * (dispatch - over_scenarios(last))
    cons_ref[...] = last[:hours]
    for o in range(1, groups):
        qcopy(o).wait_recv()
    line = qbuf[0]
    for g in range(1, groups):
        line = line + qbuf[g]
    step = (last - average)[:hours]
    line = line[:1, : ITERS + 1] / everything[:, : ITERS + 1]
    line = jnp.where(iota(line.shape, 1) == ITERS, line - jnp.sum(step * step), line)
    spread_ref[...] = line / (hours * gens)

    solved.wait()
    for i in range(ITERS + 1):
        for o in range(1, areas):
            ecopy(i, o).wait_send()
    for o in range(1, groups):
        for i in range(2):
            pcopy(i, o).wait_send()
        qcopy(o).wait_send()


def store(*refs):
    count = (len(refs) - 1) // 2
    copies = [
        pltpu.make_async_copy(refs[i], refs[count + i], refs[-1].at[i]) for i in range(count)
    ]
    for copy in copies:
        copy.start()
    for copy in copies:
        copy.wait()


def shards(areas, groups, load, start, multipliers, weights, penalty, inverse, *tables):
    scen, hours, buses = load.shape
    gens = multipliers.shape[2]
    rows = scen * hours
    load, start, multipliers = (
        x.transpose(1, 0, 2).reshape(rows, -1) for x in (load, start, multipliers)
    )
    ports, _, _, local_bus, _ = tables
    nports = ports.shape[1]
    width = local_bus.shape[1] * local_bus.shape[2]
    hp = -(-(hours + 3) // 16) * 16
    inner = width + gens
    bf, f32 = jnp.bfloat16, jnp.float32
    vmem = pl.BlockSpec(memory_space=pltpu.VMEM)
    dma = pltpu.SemaphoreType.DMA
    results = pl.pallas_call(
        functools.partial(kernel, areas, groups),
        out_shape=(
            jax.ShapeDtypeStruct(load.shape, f32),
            jax.ShapeDtypeStruct(multipliers.shape, f32),
            jax.ShapeDtypeStruct((hours, gens), f32),
            jax.ShapeDtypeStruct((1, ITERS + 1), f32),
        ),
        in_specs=[
            pl.BlockSpec(memory_space=pl.ANY),
            pl.BlockSpec(memory_space=pl.ANY),
            vmem,
            pl.BlockSpec(memory_space=pltpu.SMEM),
            vmem,
            pl.BlockSpec(memory_space=pl.ANY),
        ]
        + [vmem] * 5,
        out_specs=(pl.BlockSpec(memory_space=pl.ANY),) + (vmem,) * 3,
        scratch_shapes=[
            pltpu.VMEM((buses, buses), bf),
            pltpu.VMEM((rows, buses), f32),
            pltpu.VMEM((rows, buses), f32),
            pltpu.VMEM((rows, buses), f32),
            pltpu.VMEM((rows + width, buses), bf),
            pltpu.VMEM((rows, buses), f32),
            pltpu.VMEM((inner, buses), bf),
            pltpu.VMEM((buses, nports), bf),
            pltpu.VMEM((areas * nports, width), bf),
            pltpu.VMEM((2 * rows + inner, nports), f32),
            pltpu.VMEM((inner, gens + nports), bf),
            pltpu.VMEM((rows, gens), f32),
            pltpu.VMEM((ITERS + 1, areas, rows + hp, nports), bf),
            pltpu.VMEM((2, groups, hp, gens + nports), bf),
            pltpu.VMEM((groups, 8, 128), f32),
            dma((buses // BLOCK,)),
            dma,
            dma((2,)),
            dma((ITERS + 1, areas)),
            dma((ITERS + 1, areas)),
            dma((2, groups)),
            dma((2, groups)),
            dma((groups,)),
            dma((groups,)),
        ],
        compiler_params=pltpu.CompilerParams(collective_id=0, has_side_effects=True),
        name="hedging",
    )(load, start, multipliers, weights, penalty.reshape(1, gens), inverse, *tables)
    solved, duals, average, spread = pl.pallas_call(
        store,
        out_shape=tuple(jax.ShapeDtypeStruct(x.shape, x.dtype) for x in results),
        in_specs=[vmem] * 4,
        out_specs=(pl.BlockSpec(memory_space=pl.ANY),) * 4,
        scratch_shapes=[dma((4,))],
        name="store",
    )(*results)
    solved, duals = (
        x.reshape(hours, scen, -1).transpose(1, 0, 2) for x in (solved, duals)
    )
    return solved, duals, average, spread


def solution(mesh):
    placed = (
        P("scen", None, "area"),
        P("scen", None, "area"),
        P("scen", None, "area"),
        P("scen"),
        P("area"),
        P("area", None),
        P(),
        P(),
        P(),
        P(),
        P(),
    )
    return jax.shard_map(
        functools.partial(shards, mesh.shape["area"], mesh.shape["scen"]),
        mesh=mesh,
        in_specs=placed,
        out_specs=(
            P("scen", None, "area"),
            P("scen", None, "area"),
            P(None, "area"),
            P("area", None),
        ),
        check_vma=False,
    )
```

```python
import functools

import jax
import jax.numpy as jnp
from jax import lax
from jax.experimental import pallas as pl
from jax.experimental.pallas import tpu as pltpu
from jax.sharding import PartitionSpec as P

ITERS = 4
BLOCK = 256


def split(x):
    high = x.astype(jnp.bfloat16)
    low = (x - high.astype(jnp.float32)).astype(jnp.bfloat16)
    return high, low


def dot(a, b):
    return jnp.dot(a, b, preferred_element_type=jnp.float32)


def exact(a, b):
    total = jnp.zeros((a.shape[0], b.shape[1]), jnp.float32)
    rest, other, first = (b, a, False) if a.shape[1] == b.shape[0] and a.shape[0] > b.shape[1] else (a, b, True)
    for _ in range(3):
        piece = rest.astype(jnp.bfloat16)
        rest = rest - piece.astype(jnp.float32)
        total = total + (dot(piece, other.astype(jnp.bfloat16)) if first else dot(other.astype(jnp.bfloat16), piece))
    return total


def iota(shape, axis):
    return lax.broadcasted_iota(jnp.int32, shape, axis)


def kernel(
    areas,
    groups,
    load_hbm,
    start_hbm,
    mult_ref,
    weight_ref,
    pen_ref,
    inv_ref,
    ports_ref,
    neigh_ref,
    rport_ref,
    lbus_ref,
    susc_ref,
    sol_hbm,
    newm_ref,
    cons_ref,
    spread_ref,
    inv,
    sol_ref,
    load_ref,
    start_ref,
    left,
    full,
    h,
    pick,
    sel,
    acc,
    hsub,
    duals,
    ebuf,
    pbuf,
    qbuf,
    dma_sem,
    out_sem,
    in_sem,
    esend,
    erecv,
    psend,
    precv,
    qsend,
    qrecv,
):
    rows, buses = load_ref.shape
    gens = mult_ref.shape[1]
    scen = weight_ref.shape[0]
    hours = rows // scen
    nports = ports_ref.shape[1]
    slots, ties = lbus_ref.shape[1:]
    width = slots * ties
    hp = pbuf.shape[2]
    blocks = buses // BLOCK
    area = lax.axis_index("area")
    group = lax.axis_index("scen")

    def fetch(j):
        cols = pl.ds(pl.multiple_of(j * BLOCK, BLOCK), BLOCK)
        return pltpu.make_async_copy(inv_ref.at[:, cols], inv.at[:, cols], dma_sem.at[j])

    barrier = pltpu.get_barrier_semaphore()
    for o in range(1, areas):
        pl.semaphore_signal(
            barrier,
            inc=1,
            device_id={"area": lax.rem(area + o, areas)},
            device_id_type=pl.DeviceIdType.MESH,
        )
    for o in range(1, groups):
        pl.semaphore_signal(
            barrier,
            inc=1,
            device_id={"scen": lax.rem(group + o, groups)},
            device_id_type=pl.DeviceIdType.MESH,
        )

    load_in = pltpu.make_async_copy(load_hbm, load_ref, in_sem.at[0])
    start_in = pltpu.make_async_copy(start_hbm, start_ref, in_sem.at[1])
    start_in.start()
    load_in.start()
    for j in range(blocks):
        fetch(j).start()

    def ecopy(i, o):
        first = rows if i == ITERS else 0
        count = (rows if i == 0 else rows + hp) - first
        part = ebuf.at[i, area, pl.ds(first, count)]
        return pltpu.make_async_remote_copy(
            src_ref=part,
            dst_ref=part,
            send_sem=esend.at[i, o],
            recv_sem=erecv.at[i, o],
            device_id={"area": lax.rem(area + o, areas)},
            device_id_type=pl.DeviceIdType.MESH,
        )

    def pcopy(i, o):
        return pltpu.make_async_remote_copy(
            src_ref=pbuf.at[i, group],
            dst_ref=pbuf.at[i, group],
            send_sem=psend.at[i, o],
            recv_sem=precv.at[i, o],
            device_id={"scen": lax.rem(group + o, groups)},
            device_id_type=pl.DeviceIdType.MESH,
        )

    def qcopy(o):
        return pltpu.make_async_remote_copy(
            src_ref=qbuf.at[group],
            dst_ref=qbuf.at[group],
            send_sem=qsend.at[o],
            recv_sem=qrecv.at[o],
            device_id={"scen": lax.rem(group + o, groups)},
            device_id_type=pl.DeviceIdType.MESH,
        )

    inside = gens + nports
    seat = iota((scen, inside), 0)
    weights = jnp.zeros((scen, inside), jnp.float32)
    for s in range(scen):
        weights = jnp.where(seat == s, weight_ref[s], weights)
    weight_sum = jnp.sum(weights, axis=0, keepdims=True)
    row_id = iota((hp, inside), 0)

    def over_scenarios(x):
        return jnp.broadcast_to(x[:hours, None, :], (hours, scen, x.shape[1])).reshape(rows, x.shape[1])

    def send_sums(i, x):
        sums = jnp.sum(weights[None] * x.reshape(hours, scen, inside), axis=1)
        sums = jnp.concatenate((sums, jnp.zeros((hp - hours, inside), jnp.float32)), axis=0)
        if i == 0:
            rest = weight_sum
            for r in range(hours, hours + 3):
                piece = rest.astype(jnp.bfloat16).astype(jnp.float32)
                sums = jnp.where(row_id == r, piece, sums)
                rest = rest - piece
        pbuf[i, group] = sums.astype(jnp.bfloat16)
        for o in range(1, groups):
            pcopy(i, o).start()

    def get_sums(i):
        for o in range(1, groups):
            pcopy(i, o).wait_recv()
        total = pbuf[i, 0].astype(jnp.float32)
        for g in range(1, groups):
            total = total + pbuf[i, g].astype(jnp.float32)
        return total

    def squares(x, center):
        off = x - over_scenarios(center)
        off = off.reshape(hours, scen, gens)
        return jnp.sum(weights[None, :, :gens] * off * off)

    def send_exchange(i):
        for o in range(1, areas):
            ecopy(i, o).start()

    pick[...] = jnp.where(
        iota((buses, nports), 0) == ports_ref[pl.ds(area, 1), :], 1.0, 0.0
    ).astype(jnp.bfloat16)
    start_in.wait()
    start_b = start_ref[...].astype(jnp.bfloat16)
    dispatch = start_ref[:, :gens]
    offered = dot(start_b, pick[...])
    pl.semaphore_wait(barrier, areas + groups - 2)
    ebuf[0, area, :rows, :] = offered.astype(jnp.bfloat16)
    send_exchange(0)
    send_sums(0, jnp.concatenate((dispatch, offered), axis=1))

    def to_row(x):
        spread_out = exact(x, jnp.where(iota((ties, width), 1) % ties == iota((ties, width), 0), 1.0, 0.0))
        mine = iota((slots, width), 1) // ties == iota((slots, width), 0)
        return jnp.sum(jnp.where(mine, spread_out, 0.0), axis=0, keepdims=True)

    susc = to_row(susc_ref[area])
    rport = to_row(rport_ref[area].astype(jnp.float32))
    neigh = exact(
        neigh_ref[pl.ds(area, 1), :].astype(jnp.float32),
        jnp.where(iota((slots, width), 1) // ties == iota((slots, width), 0), 1.0, 0.0),
    )
    code = neigh * nports + rport
    sel[...] = jnp.where(
        iota((areas * nports, width), 0).astype(jnp.float32) == code, 1.0, 0.0
    ).astype(jnp.bfloat16)
    stretched = exact(
        jnp.where(iota((width, slots), 0) // ties == iota((width, slots), 1), 1.0, 0.0),
        lbus_ref[area].astype(jnp.float32),
    )
    mine = iota((width, ties), 0) % ties == iota((width, ties), 1)
    bus_col = jnp.sum(jnp.where(mine, stretched, 0.0), axis=1, keepdims=True)
    left[rows:, :] = jnp.where(
        iota((width, buses), 1).astype(jnp.float32) == bus_col, 1.0, 0.0
    ).astype(jnp.bfloat16)
    load_in.wait()
    left[:rows, :] = load_ref[...].astype(jnp.bfloat16)

    acc[...] = jnp.zeros_like(acc)

    def column_block(j, carry):
        fetch(j).wait()
        cols = pl.ds(pl.multiple_of(j * BLOCK, BLOCK), BLOCK)
        product = dot(left[...], inv[:, cols])
        own = product[:rows]
        full[:, cols] = own
        h[:width, cols] = product[rows:].astype(jnp.bfloat16)
        h[width:, cols] = inv[:gens, cols]
        high, low = split(own)
        stack = jnp.concatenate((high, low, h[:, cols]), axis=0)
        acc[...] += dot(stack, pick[cols, :])
        return carry

    lax.fori_loop(0, blocks, column_block, 0)

    base = jnp.concatenate((full[:, :gens], acc[:rows] + acc[rows : 2 * rows]), axis=1)
    hsub[...] = jnp.concatenate(
        (h[:, :gens], acc[2 * rows :].astype(jnp.bfloat16)), axis=1
    )
    pen = pen_ref[...]

    def through(source, first, count):
        high, low = split(source)
        part = hsub[first : first + count, :]
        return dot(high, part) + dot(low, part)

    def arrived(i, first, count):
        for o in range(1, areas):
            ecopy(i, o).wait_recv()
        received = dot(ebuf[i, 0, first : first + count, :], sel[:nports, :])
        for b in range(1, areas):
            received = received + dot(
                ebuf[i, b, first : first + count, :], sel[b * nports : (b + 1) * nports, :]
            )
        received = received * susc
        return received, dot(received.astype(jnp.bfloat16), hsub[:width, :])

    still = base - through(mult_ref[...], width, gens)
    send_sums(1, still)
    total = get_sums(0)
    everything = total[hours : hours + 1, :]
    for r in range(hours + 1, hours + 3):
        everything = everything + total[r : r + 1, :]
    mean = jnp.where(row_id < hours, total / everything, 0.0)
    duals[...] = mult_ref[...]
    numerators = []
    before = still
    for i in range(ITERS):
        received, added = arrived(i, 0, rows if i == 0 else rows + hp)
        if i > 0:
            if i == 1:
                still_mean = get_sums(1) / everything
            mean = still_mean + pull + added[rows:]
        average = mean[:, :gens]
        if i == ITERS - 1:
            ebuf[ITERS, area, rows:, :] = mean[:, gens:].astype(jnp.bfloat16)
            send_exchange(ITERS)
        pull = through(pen * average, width, gens)
        update = before + added[:rows] + over_scenarios(pull if i == 0 else pull + pull)
        previous, dispatch = dispatch, update[:, :gens]
        if i < ITERS - 1:
            ebuf[i + 1, area, :rows, :] = update[:, gens:].astype(jnp.bfloat16)
            ebuf[i + 1, area, rows:, :] = mean[:, gens:].astype(jnp.bfloat16)
            send_exchange(i + 1)
        if i > 0:
            duals[...] = duals[...] + pen * (previous - over_scenarios(average))
        numerators.append(squares(previous, average))
        if i < ITERS - 1:
            before = base - through(duals[...] + pen * dispatch, width, gens)

    numerators.append(squares(dispatch, average))
    lane = iota(qbuf.shape[1:], 1)
    line = jnp.zeros(qbuf.shape[1:], jnp.float32)
    for i, value in enumerate(numerators):
        line = jnp.where(lane == i, value, line)
    qbuf[group] = line
    for o in range(1, groups):
        qcopy(o).start()

    hedge = over_scenarios(pen * average) - duals[...]
    high = jnp.concatenate((received[:rows], hedge), axis=1).astype(jnp.bfloat16)
    sol_ref[:, :gens] = dispatch
    for j in range(gens // BLOCK, blocks):
        cols = slice(j * BLOCK, (j + 1) * BLOCK)
        sol_ref[:, cols] = full[:, cols] + dot(high, h[:, cols])

    solved = pltpu.make_async_copy(sol_ref, sol_hbm, out_sem)
    solved.start()

    _, added = arrived(ITERS, rows, hp)
    last = (still_mean + pull + added)[:, :gens]
    newm_ref[...] = duals[...] + pen * (dispatch - over_scenarios(last))
    cons_ref[...] = last[:hours]
    for o in range(1, groups):
        qcopy(o).wait_recv()
    line = qbuf[0]
    for g in range(1, groups):
        line = line + qbuf[g]
    step = (last - average)[:hours]
    line = line[:1, : ITERS + 1] / everything[:, : ITERS + 1]
    line = jnp.where(iota(line.shape, 1) == ITERS, line - jnp.sum(step * step), line)
    spread_ref[...] = line / (hours * gens)

    solved.wait()
    for i in range(ITERS + 1):
        for o in range(1, areas):
            ecopy(i, o).wait_send()
    for o in range(1, groups):
        for i in range(2):
            pcopy(i, o).wait_send()
        qcopy(o).wait_send()


def store(*refs):
    count = (len(refs) - 1) // 2
    copies = [
        pltpu.make_async_copy(refs[i], refs[count + i], refs[-1].at[i]) for i in range(count)
    ]
    for copy in copies:
        copy.start()
    for copy in copies:
        copy.wait()


def shards(areas, groups, load, start, multipliers, weights, penalty, inverse, *tables):
    scen, hours, buses = load.shape
    gens = multipliers.shape[2]
    rows = scen * hours
    load, start, multipliers = (
        x.transpose(1, 0, 2).reshape(rows, -1) for x in (load, start, multipliers)
    )
    ports, _, _, local_bus, _ = tables
    nports = ports.shape[1]
    width = local_bus.shape[1] * local_bus.shape[2]
    hp = -(-(hours + 3) // 16) * 16
    inner = width + gens
    bf, f32 = jnp.bfloat16, jnp.float32
    vmem = pl.BlockSpec(memory_space=pltpu.VMEM)
    dma = pltpu.SemaphoreType.DMA
    results = pl.pallas_call(
        functools.partial(kernel, areas, groups),
        out_shape=(
            jax.ShapeDtypeStruct(load.shape, f32),
            jax.ShapeDtypeStruct(multipliers.shape, f32),
            jax.ShapeDtypeStruct((hours, gens), f32),
            jax.ShapeDtypeStruct((1, ITERS + 1), f32),
        ),
        in_specs=[
            pl.BlockSpec(memory_space=pl.ANY),
            pl.BlockSpec(memory_space=pl.ANY),
            vmem,
            pl.BlockSpec(memory_space=pltpu.SMEM),
            vmem,
            pl.BlockSpec(memory_space=pl.ANY),
        ]
        + [vmem] * 5,
        out_specs=(pl.BlockSpec(memory_space=pl.ANY),) + (vmem,) * 3,
        scratch_shapes=[
            pltpu.VMEM((buses, buses), bf),
            pltpu.VMEM((rows, buses), f32),
            pltpu.VMEM((rows, buses), f32),
            pltpu.VMEM((rows, buses), f32),
            pltpu.VMEM((rows + width, buses), bf),
            pltpu.VMEM((rows, buses), f32),
            pltpu.VMEM((inner, buses), bf),
            pltpu.VMEM((buses, nports), bf),
            pltpu.VMEM((areas * nports, width), bf),
            pltpu.VMEM((2 * rows + inner, nports), f32),
            pltpu.VMEM((inner, gens + nports), bf),
            pltpu.VMEM((rows, gens), f32),
            pltpu.VMEM((ITERS + 1, areas, rows + hp, nports), bf),
            pltpu.VMEM((2, groups, hp, gens + nports), bf),
            pltpu.VMEM((groups, 8, 128), f32),
            dma((buses // BLOCK,)),
            dma,
            dma((2,)),
            dma((ITERS + 1, areas)),
            dma((ITERS + 1, areas)),
            dma((2, groups)),
            dma((2, groups)),
            dma((groups,)),
            dma((groups,)),
        ],
        compiler_params=pltpu.CompilerParams(collective_id=0, has_side_effects=True),
        name="hedging",
    )(load, start, multipliers, weights, penalty.reshape(1, gens), inverse, *tables)
    solved, duals, average, spread = pl.pallas_call(
        store,
        out_shape=tuple(jax.ShapeDtypeStruct(x.shape, x.dtype) for x in results),
        in_specs=[vmem] * 4,
        out_specs=(pl.BlockSpec(memory_space=pl.ANY),) * 4,
        scratch_shapes=[dma((4,))],
        name="store",
    )(*results)
    solved, duals = (
        x.reshape(hours, scen, -1).transpose(1, 0, 2) for x in (solved, duals)
    )
    return solved, duals, average, spread


def solution(mesh):
    placed = (
        P("scen", None, "area"),
        P("scen", None, "area"),
        P("scen", None, "area"),
        P("scen"),
        P("area"),
        P("area", None),
        P(),
        P(),
        P(),
        P(),
        P(),
    )
    return jax.shard_map(
        functools.partial(shards, mesh.shape["area"], mesh.shape["scen"]),
        mesh=mesh,
        in_specs=placed,
        out_specs=(
            P("scen", None, "area"),
            P("scen", None, "area"),
            P(None, "area"),
            P("area", None),
        ),
        check_vma=False,
    )
```
